32 devices in a mesh: slab: 2 (over y), strip: 16 (over z, x, core).
Axes of the slice: x: 2, y: 2, z: 4, core: 2. Of those that a mesh axis runs over, the one named last changes fastest.
Arguments:
- volume: bfloat16 [8, 512, 1024], P('slab', 'strip'), may hold values from -1 to 1
- shear: int32 [2, 8], P(None, 'slab'), may hold values from -64 to 64, as said below
- probe: float32 [2, 128, 128], replicated, may hold values from -4 to 4
- positions: int32 [2, 16, 16, 2], P('slab', 'strip'), may hold values from -64 to 192, as said below
- measured: bfloat16 [2, 16, 16, 128, 128], P('slab', 'strip'), may hold values from 0.099609375 to 4
Outputs:
- volume_grad: bfloat16 [8, 512, 1024], P('slab', 'strip')
The draws below stay inside these ranges and needn't reach their ends.
Inputs may be any that keep to these rules, and one draw needn't show every extreme that they name: shear[v, z] is the floor of s_v (2 ((z + r_v) mod 8) - 8) / 8 for integers s_v from -64 to 64 and r_v from 0 to 7. `positions`: row offsets (last index 0) lie from -64 to 192, column offsets (last index 1) from -64 to 64, so every patch lies within 64 pixels of its tile.
All inputs are finite; a program needn't handle non-finite values.
Results may differ from the reference program's by a relative error of at most 0.023.
Values may be sent and summed in bfloat16 or wider, within the bound.
A program may use at most 64 MiB of HBM per device.

```python
import math
import jax
import jax.numpy as jnp
from jax import lax

X = 1024
TILE_W = 128
PATCH = 128
SHEAR = 64
DEPTH_DEV = 4
PPT = 16
DEPTH = 8
ROWS = 512
VIEWS = 2
TILES = 16
TILE_ROWS = 256
RIM = 64
N_SLAB = 2


def draw_shear(key, part):
    slope_key, sign_key, turn_key = jax.random.split(jax.random.fold_in(key, 3), 3)
    slopes = jax.random.randint(slope_key, (VIEWS,), -SHEAR, SHEAR + 1)
    flipped = 2 * jax.random.randint(sign_key, (), 0, 2) - 1
    slopes = slopes.at[0].set(flipped * SHEAR).at[1].set(-flipped * SHEAR)
    turns = jax.random.randint(turn_key, (VIEWS,), 0, DEPTH)
    depth_index = jnp.arange(DEPTH, dtype=jnp.int32)
    rotated = (depth_index[None, :] + turns[:, None]) % DEPTH
    return (slopes[:, None] * (2 * rotated - DEPTH) // DEPTH).astype(jnp.int32)


def draw_positions(key, part):
    row_key, col_key = jax.random.split(jax.random.fold_in(key, 7))
    shape = (VIEWS, TILES, PPT)
    rows_off = jax.random.randint(row_key, shape, -RIM, TILE_ROWS - RIM + 1)
    cols_off = jax.random.randint(col_key, shape, -RIM, TILE_W - RIM + 1)
    rows_off = rows_off.at[0, 0, 0].set(-RIM).at[0, 0, 1].set(TILE_ROWS - RIM)
    return jnp.stack([rows_off, cols_off], axis=-1).astype(jnp.int32)


def block_scale(stream_key, shape, cuts, least, high):
    def one(axis_at, shards_of):
        steps = jax.random.uniform(jax.random.fold_in(jax.random.fold_in(stream_key, 6), axis_at), (shards_of,), jnp.float32, least / len(cuts), high / len(cuts))
        return jnp.repeat(jnp.exp(steps), shape[axis_at] // shards_of).reshape((-1,) + (1,) * (len(shape) - axis_at - 1))

    level = one(*cuts[0])
    for cut in cuts[1:]:
        level = level * one(*cut)
    return level


def scatter_about(stream_key, dims, spread, reach, pieces=(), kind=jnp.bfloat16):
    values = spread * jax.random.normal(stream_key, dims, jnp.float32)
    if pieces:
        values = values * block_scale(stream_key, dims, pieces, -0.22, 0.18)
    return jnp.clip(values, -reach, reach).astype(kind)


def setup_inputs(seed: int = 0) -> dict:
    key_list = jax.random.split(jax.random.key(seed), 6)
    volume = scatter_about(key_list[0], (DEPTH, ROWS, X), 0.15, 1.0, ((0, 2), (1, 16)))
    shear = draw_shear(jax.random.fold_in(key_list[5], 71), 0)
    probe = scatter_about(key_list[2], (2, PATCH, PATCH), 0.7, 4.0, (), jnp.float32)
    positions = draw_positions(jax.random.fold_in(key_list[5], 71), 0)
    measured = jnp.clip(jnp.exp(math.log(4.0) - 3.6927934 * jax.random.uniform(key_list[4], (VIEWS, TILES, PPT, PATCH, PATCH), jnp.float32) ** block_scale(key_list[4], (VIEWS, TILES, PPT, PATCH, PATCH), ((0, 2), (1, 16)), -0.2, 0.2)), 0.099609375, 4.0).astype(jnp.bfloat16)
    return dict(volume=volume, shear=shear, probe=probe, positions=positions, measured=measured)


grad_scale = 0.125


def shear_sum(volume_block, shear_block):
    padded = jnp.pad(volume_block.astype(jnp.float32), ((0, 0), (0, 0), (SHEAR, SHEAR)))

    def step(grand_sum, item):
        layer, shifts = item

        def shifted(shift):
            return lax.dynamic_slice_in_dim(layer, (SHEAR - shift).astype(jnp.int32), X, 1)

        return grand_sum + jax.vmap(shifted)(shifts), None

    start = jnp.zeros((shear_block.shape[0], volume_block.shape[1], X), jnp.float32)
    grand_sum, _ = lax.scan(step, start, (padded, shear_block.T))
    return grand_sum


def patch_grads(phase, probe, measured):
    cos_o = jnp.cos(phase)
    sin_o = jnp.sin(phase)
    probe_re = probe[0]
    probe_im = probe[1]
    wave = (probe_re * cos_o - probe_im * sin_o) + 1j * (probe_re * sin_o + probe_im * cos_o)
    far = jnp.fft.fft2(wave, norm="ortho")
    resid = jnp.real(far) ** 2 + jnp.imag(far) ** 2 - measured.astype(jnp.float32)
    back = jnp.fft.ifft2((grad_scale * resid) * far, norm="ortho")
    back_re = jnp.real(back)
    back_im = jnp.imag(back)
    grad_re = probe_re * back_re + probe_im * back_im
    grad_im = probe_re * back_im - probe_im * back_re
    return cos_o * grad_im - sin_o * grad_re


def reference(volume, shear, probe, positions, measured):
    col_tiles = X // TILE_W
    vol_slabs = volume.reshape(N_SLAB, DEPTH_DEV, ROWS, X)
    shear_slabs = jnp.transpose(shear.reshape(VIEWS, N_SLAB, DEPTH_DEV), (1, 0, 2))

    def slab_term(grand_sum, item):
        term = lax.optimization_barrier(shear_sum(item[0], item[1]).astype(jnp.bfloat16))
        return grand_sum + term.astype(jnp.float32), None

    projection, _ = lax.scan(slab_term, jnp.zeros((VIEWS, ROWS, X), jnp.float32), (vol_slabs, shear_slabs))
    padded_proj = jnp.pad(projection, ((0, 0), (RIM, RIM), (RIM, RIM)))

    def tile_step(grad_field, flat):
        view = flat // TILES
        tile = flat % TILES
        row_zero = (tile // col_tiles) * TILE_ROWS + RIM
        col_zero = (tile % col_tiles) * TILE_W + RIM
        field = lax.dynamic_index_in_dim(padded_proj, view, 0, keepdims=False)
        corners = positions[view, tile]

        def cut(corner):
            return lax.dynamic_slice(field, (row_zero + corner[0], col_zero + corner[1]), (PATCH, PATCH))

        phases = jax.vmap(cut)(corners)
        grads = patch_grads(phases, probe, measured[view, tile])

        def add_one(index, acc):
            corner = corners[index]
            start = (view, row_zero + corner[0], col_zero + corner[1])
            current = lax.dynamic_slice(acc, start, (1, PATCH, PATCH))
            return lax.dynamic_update_slice(acc, current + grads[index][None], start)

        return lax.fori_loop(0, PPT, add_one, grad_field), None

    start_field = jnp.zeros((VIEWS, ROWS + 2 * RIM, X + 2 * RIM), jnp.float32)
    grad_field, _ = lax.scan(tile_step, start_field, jnp.arange(VIEWS * TILES, dtype=jnp.int32))
    object_grad = grad_field[:, RIM:RIM + ROWS, RIM:RIM + X].astype(jnp.bfloat16)
    padded_grad = jnp.pad(object_grad, ((0, 0), (0, 0), (SHEAR, SHEAR)))

    def layer(shifts):
        def shifted(field, shift):
            return lax.dynamic_slice_in_dim(field, (SHEAR + shift).astype(jnp.int32), X, 1).astype(jnp.float32)

        return jnp.sum(jax.vmap(shifted)(padded_grad, shifts), axis=0).astype(jnp.bfloat16)

    return lax.map(layer, shear.T)
```

```python
import functools
import math

import jax
import jax.numpy as jnp
import numpy as np
from jax import lax
from jax.experimental import pallas as pl
from jax.experimental.pallas import tpu as pltpu
from jax.sharding import PartitionSpec as P

TILE_W = 128
PATCH = 128
RIM = PATCH // 2
WIN = TILE_W + 2 * RIM
GRAD_SCALE = 0.125
MESH = pl.DeviceIdType.MESH
F32 = jnp.float32
BF16 = jnp.bfloat16


def dft_tables():
    index = np.arange(PATCH)
    angle = 2.0 * math.pi * ((index[:, None] * index[None, :]) % PATCH) / PATCH
    cosine = np.cos(angle) / math.sqrt(PATCH)
    sine = np.sin(angle) / math.sqrt(PATCH)
    first = np.block([[cosine, -sine], [sine, cosine]])
    out = []
    for table in (first, first.T):
        high = table.astype(BF16)
        out.append(high)
        out.append((table - high.astype(np.float64)).astype(BF16))
    return np.stack(out)


def place():
    slab = lax.axis_index("slab")
    strip = lax.axis_index("strip")
    return slab, strip


def greet(slab, strip, slabs, strips, col_tiles, edge):
    group, col = strip // col_tiles, strip % col_tiles
    groups = strips // col_tiles
    barrier = pltpu.get_barrier_semaphore()

    def signal(to_slab, to_strip):
        pl.semaphore_signal(
            barrier, inc=1, device_id={"slab": to_slab, "strip": to_strip}, device_id_type=MESH
        )

    for step in range(1, slabs):
        signal(lax.rem(slab + step, slabs), strip)
    for step in range(1, col_tiles):
        signal(slab, group * col_tiles + lax.rem(col + step, col_tiles))

    def greet_group(other, near, far_first):
        @pl.when(near)
        def _():
            for tile in range(col_tiles):
                signal(slab, other * col_tiles + tile)

        @pl.when(jnp.logical_not(near))
        def _():
            for tile in range(edge):
                signal(slab, other * col_tiles + far_first + tile)

    @pl.when(group > 0)
    def _():
        greet_group(group - 1, col < edge, col_tiles - edge)

    @pl.when(group < groups - 1)
    def _():
        greet_group(group + 1, col >= col_tiles - edge, 0)

    base = slabs - 1 + col_tiles - 1
    above = jnp.where(group > 0, jnp.where(col < edge, col_tiles, edge), 0)
    below = jnp.where(group < groups - 1, jnp.where(col >= col_tiles - edge, col_tiles, edge), 0)
    return barrier, base + above + below


def field_kernel(
    slabs, strips, shear_ref, vol_ref, ext_ref,
    part, slab_in, proj, land, land_edge,
    slab_send, slab_recv, send, recv, edge_send, edge_recv,
):
    depth, rows, width = vol_ref.shape
    wide = width + 2 * RIM
    col_tiles = width // TILE_W
    groups = strips // col_tiles
    edge = RIM // rows
    slab, strip = place()
    group, col = strip // col_tiles, strip % col_tiles
    barrier, peers = greet(slab, strip, slabs, strips, col_tiles, edge)
    lane = lax.broadcasted_iota(jnp.int32, (rows, wide), 1)
    inside = (lane >= RIM) & (lane < RIM + width)
    zeros = jnp.zeros((rows, 2 * RIM), F32)

    def partial(view):
        total = jnp.zeros((rows, wide), F32)
        for z in range(depth):
            layer = jnp.concatenate([vol_ref[z].astype(F32), zeros], 1)
            total = total + pltpu.roll(layer, shear_ref[view, z] + RIM, 1)
        return jnp.where(inside, total, 0.0).astype(BF16)

    copies = []
    for step in range(1, slabs):
        view = lax.rem(slab + step, slabs)
        part[step - 1] = partial(view)
        if step == 1:
            pl.semaphore_wait(barrier, peers)
        copy = pltpu.make_async_remote_copy(
            src_ref=part.at[step - 1], dst_ref=slab_in.at[step - 1],
            send_sem=slab_send.at[step - 1], recv_sem=slab_recv.at[step - 1],
            device_id={"slab": view, "strip": strip}, device_id_type=MESH,
        )
        copy.start()
        copies.append(copy)
    total = partial(slab).astype(F32)
    if slabs == 1:
        pl.semaphore_wait(barrier, peers)
    for step in range(1, slabs):
        copies[step - 1].wait_recv()
        total = total + slab_in[step - 1].astype(F32)
    proj[...] = total.astype(BF16)

    def window(tile):
        return pl.ds(pl.multiple_of(tile * TILE_W, TILE_W), WIN)

    top = (col < edge) & (group > 0)
    bottom = (col >= col_tiles - edge) & (group < groups - 1)
    other = jnp.where(col < edge, group - 1, group + 1)
    slot = jnp.where(col < edge, edge + col, col - (col_tiles - edge))

    def edge_copy(tile):
        return pltpu.make_async_remote_copy(
            src_ref=proj.at[:, pl.ds(tile * TILE_W, WIN)], dst_ref=land_edge.at[slot],
            send_sem=edge_send.at[tile], recv_sem=edge_recv.at[slot],
            device_id={"slab": slab, "strip": other * col_tiles + tile}, device_id_type=MESH,
        )

    @pl.when(top | bottom)
    def _():
        for tile in range(col_tiles):
            edge_copy(tile).start()

    group_copies = []
    for step in range(1, col_tiles):
        tile = lax.rem(col + step, col_tiles)
        copy = pltpu.make_async_remote_copy(
            src_ref=proj.at[:, window(tile)], dst_ref=land.at[step - 1],
            send_sem=send.at[step - 1], recv_sem=recv.at[step - 1],
            device_id={"slab": slab, "strip": group * col_tiles + tile}, device_id_type=MESH,
        )
        copy.start()
        group_copies.append(copy)
    ext_ref[edge + col] = proj[:, window(col)]
    for step in range(1, col_tiles):
        group_copies[step - 1].wait_recv()
        ext_ref[edge + lax.rem(col + col_tiles - step, col_tiles)] = land[step - 1]

    def edge_in(first, place_at, has):
        @pl.when(has)
        def _():
            for k in range(edge):
                pltpu.make_async_remote_copy(
                    src_ref=proj.at[:, pl.ds(0, WIN)], dst_ref=land_edge.at[first + k],
                    send_sem=edge_send.at[0], recv_sem=edge_recv.at[first + k],
                    device_id={"slab": slab, "strip": other * col_tiles}, device_id_type=MESH,
                ).wait_recv()
                ext_ref[place_at + k] = land_edge[first + k]

        @pl.when(jnp.logical_not(has))
        def _():
            for k in range(edge):
                ext_ref[place_at + k] = jnp.zeros((rows, WIN), BF16)

    edge_in(0, 0, group > 0)
    edge_in(edge, edge + col_tiles, group < groups - 1)
    for copy in copies:
        copy.wait_send()
    for copy in group_copies:
        copy.wait_send()

    @pl.when(top | bottom)
    def _():
        for tile in range(col_tiles):
            edge_copy(tile).wait_send()


def cos_sin(x):
    turn = jnp.floor(x * (2.0 / math.pi) + 0.5)
    r = ((x - turn * 1.5703125) - turn * 4.837512969970703125e-4) - turn * 7.54978995489188216e-8
    z = r * r
    s = ((-1.9515295891e-4 * z + 8.3321608736e-3) * z - 1.6666654611e-1) * z * r + r
    c = ((2.443315711809948e-5 * z - 1.388731625493765e-3) * z + 4.166664568298827e-2) * z * z
    c = c - 0.5 * z + 1.0
    quarter = turn.astype(jnp.int32) & 3
    odd = (quarter & 1) == 1
    cos = jnp.where(odd, s, c)
    sin = jnp.where(odd, c, s)
    cos = jnp.where((quarter == 1) | (quarter == 2), -cos, cos)
    sin = jnp.where(quarter >= 2, -sin, sin)
    return cos, sin


def split(x):
    high = x.astype(BF16)
    return high, (x - high.astype(F32)).astype(BF16)


def mm(a, b):
    return jnp.dot(a, b, preferred_element_type=F32)


def patch_kernel(pos_ref, ext_ref, probe_ref, meas_ref, tab_ref, out_ref, cosf, sinf, acc):
    slots, rows, _ = ext_ref.shape
    count = meas_ref.shape[0]
    halves = WIN // PATCH

    def right(x, which):
        high, low = split(x)
        t_high, t_low = tab_ref[2 * which], tab_ref[2 * which + 1]
        return mm(high, t_high) + (mm(low, t_high) + mm(high, t_low))

    def left(which, x):
        high, low = split(x)
        t_high, t_low = tab_ref[2 * which], tab_ref[2 * which + 1]
        return mm(t_high, high) + (mm(t_high, low) + mm(t_low, high))

    def trig(j, _):
        cos, sin = cos_sin(ext_ref[j].astype(F32))
        at = pl.ds(pl.multiple_of(j * rows, rows), rows)
        for h in range(halves):
            cosf[h, at, :] = cos[:, h * PATCH : (h + 1) * PATCH]
            sinf[h, at, :] = sin[:, h * PATCH : (h + 1) * PATCH]
            acc[h, at, :] = jnp.zeros((rows, PATCH), F32)
        return 0

    lax.fori_loop(0, slots, trig, 0)

    def cut(field, row, by):
        strips = [field[h, pl.ds(row, PATCH), :] for h in range(halves)]
        return pltpu.roll(jnp.concatenate(strips, 1), by, 1)[:, :PATCH]

    def pair(i, _):
        probe_re, probe_im = probe_ref[0], probe_ref[1]
        where, waves, cuts = [], [], []
        for k in range(2):
            row = pos_ref[2 * i + k, 0] + RIM
            lane = pos_ref[2 * i + k, 1] + RIM
            back_by = (WIN - lane) & (WIN - 1)
            cos = cut(cosf, row, back_by)
            sin = cut(sinf, row, back_by)
            where.append((row, lane))
            cuts.append((cos, sin))
            waves.append(
                jnp.concatenate(
                    [probe_re * cos - probe_im * sin, probe_re * sin + probe_im * cos], 1
                )
            )
        half = right(jnp.concatenate(waves, 0), 0)
        half = jnp.concatenate(
            [
                jnp.concatenate([half[:PATCH, :PATCH], half[PATCH:, :PATCH]], 1),
                jnp.concatenate([half[:PATCH, PATCH:], half[PATCH:, PATCH:]], 1),
            ],
            0,
        )
        far = left(1, half)
        far_re, far_im = far[:PATCH], far[PATCH:]
        meas = jnp.concatenate([meas_ref[2 * i], meas_ref[2 * i + 1]], 1).astype(F32)
        weight = GRAD_SCALE * (far_re * far_re + far_im * far_im - meas)
        half = left(0, jnp.concatenate([weight * far_re, weight * far_im], 0))
        half = jnp.concatenate(
            [
                jnp.concatenate([half[:PATCH, :PATCH], half[PATCH:, :PATCH]], 1),
                jnp.concatenate([half[:PATCH, PATCH:], half[PATCH:, PATCH:]], 1),
            ],
            0,
        )
        back = right(half, 1)
        for k in range(2):
            row, lane = where[k]
            cos, sin = cuts[k]
            back_re = back[k * PATCH : (k + 1) * PATCH, :PATCH]
            back_im = back[k * PATCH : (k + 1) * PATCH, PATCH:]
            grad_re = probe_re * back_re + probe_im * back_im
            grad_im = probe_re * back_im - probe_im * back_re
            grad = cos * grad_im - sin * grad_re
            grad = jnp.concatenate([grad, jnp.zeros_like(grad)], 1)
            at = pl.ds(row, PATCH)
            grad = pltpu.roll(grad, lane, 1)
            for h in range(halves):
                acc[h, at, :] = acc[h, at, :] + grad[:, h * PATCH : (h + 1) * PATCH]
        return 0

    lax.fori_loop(0, count // 2, pair, 0)

    def finish(j, _):
        at = pl.ds(pl.multiple_of(j * rows, rows), rows)
        out_ref[j] = jnp.concatenate([acc[h, at, :] for h in range(halves)], 1).astype(BF16)
        return 0

    lax.fori_loop(0, slots, finish, 0)


def back_kernel(
    slabs, strips, shear_ref, grad_ref, out_ref,
    land, land_edge, total, own, slab_in,
    slab_send, slab_recv, send, recv, edge_send, edge_recv,
):
    depth, rows, width = out_ref.shape
    wide = width + 2 * RIM
    col_tiles = width // TILE_W
    groups = strips // col_tiles
    edge = RIM // rows
    slab, strip = place()
    group, col = strip // col_tiles, strip % col_tiles
    barrier, peers = greet(slab, strip, slabs, strips, col_tiles, edge)
    pl.semaphore_wait(barrier, peers)

    def edge_copy(k, other, source, owner):
        return pltpu.make_async_remote_copy(
            src_ref=grad_ref.at[source], dst_ref=land_edge.at[col],
            send_sem=edge_send.at[k], recv_sem=edge_recv.at[col],
            device_id={"slab": slab, "strip": other * col_tiles + owner}, device_id_type=MESH,
        )

    def edge_copies(act):
        @pl.when(group > 0)
        def _():
            for k in range(edge):
                act(edge_copy(k, group - 1, k, col_tiles - edge + k))

        @pl.when(group < groups - 1)
        def _():
            for k in range(edge):
                act(edge_copy(edge + k, group + 1, edge + col_tiles + k, k))

    edge_copies(lambda copy: copy.start())
    group_copies = []
    for step in range(1, col_tiles):
        tile = lax.rem(col + step, col_tiles)
        copy = pltpu.make_async_remote_copy(
            src_ref=grad_ref.at[edge + tile], dst_ref=land.at[step - 1],
            send_sem=send.at[step - 1], recv_sem=recv.at[step - 1],
            device_id={"slab": slab, "strip": group * col_tiles + tile}, device_id_type=MESH,
        )
        copy.start()
        group_copies.append(copy)
    total[...] = jnp.zeros((rows, wide), F32)

    def window(tile):
        return pl.ds(pl.multiple_of(tile * TILE_W, TILE_W), WIN)

    total[:, window(col)] = total[:, window(col)] + grad_ref[edge + col].astype(F32)
    for step in range(1, col_tiles):
        group_copies[step - 1].wait_recv()
        at = window(lax.rem(col + col_tiles - step, col_tiles))
        total[:, at] = total[:, at] + land[step - 1].astype(F32)

    has_edge = ((col < edge) & (group > 0)) | ((col >= col_tiles - edge) & (group < groups - 1))
    other = jnp.where(col < edge, group - 1, group + 1)

    @pl.when(has_edge)
    def _():
        for tile in range(col_tiles):
            pltpu.make_async_remote_copy(
                src_ref=grad_ref.at[0], dst_ref=land_edge.at[tile],
                send_sem=edge_send.at[0], recv_sem=edge_recv.at[tile],
                device_id={"slab": slab, "strip": other * col_tiles + tile}, device_id_type=MESH,
            ).wait_recv()
            at = window(tile)
            total[:, at] = total[:, at] + land_edge[tile].astype(F32)

    lane = lax.broadcasted_iota(jnp.int32, (rows, wide), 1)
    inside = (lane >= RIM) & (lane < RIM + width)
    mine = jnp.where(inside, total[...], 0.0).astype(BF16)
    own[...] = mine
    copies = []
    for step in range(1, slabs):
        copy = pltpu.make_async_remote_copy(
            src_ref=own, dst_ref=slab_in.at[step - 1],
            send_sem=slab_send.at[step - 1], recv_sem=slab_recv.at[step - 1],
            device_id={"slab": lax.rem(slab + step, slabs), "strip": strip}, device_id_type=MESH,
        )
        copy.start()
        copies.append(copy)

    def sheared(field, view, z):
        by = lax.rem(wide - RIM - shear_ref[view, z], wide)
        return pltpu.roll(field, by, 1)[:, :width]

    results = [sheared(mine.astype(F32), slab, z) for z in range(depth)]
    for step in range(1, slabs):
        copies[step - 1].wait_recv()
        field = slab_in[step - 1].astype(F32)
        view = lax.rem(slab + slabs - step, slabs)
        results = [results[z] + sheared(field, view, z) for z in range(depth)]
    for z in range(depth):
        out_ref[z] = results[z].astype(BF16)
    for copy in copies:
        copy.wait_send()
    for copy in group_copies:
        copy.wait_send()
    edge_copies(lambda copy: copy.wait_send())


def local(slabs, strips, volume, shear, probe, positions, measured):
    depth, rows, width = volume.shape
    col_tiles = width // TILE_W
    wide = width + 2 * RIM
    edge = RIM // rows
    slots = col_tiles + 2 * edge
    others = max(slabs - 1, 1)
    vmem = pl.BlockSpec(memory_space=pltpu.VMEM)
    smem = pl.BlockSpec(memory_space=pltpu.SMEM)
    dma = pltpu.SemaphoreType.DMA
    ext = pl.pallas_call(
        functools.partial(field_kernel, slabs, strips),
        out_shape=jax.ShapeDtypeStruct((slots, rows, WIN), BF16),
        in_specs=[smem, vmem],
        out_specs=vmem,
        scratch_shapes=[
            pltpu.VMEM((others, rows, wide), BF16),
            pltpu.VMEM((others, rows, wide), BF16),
            pltpu.VMEM((rows, wide), BF16),
            pltpu.VMEM((col_tiles - 1, rows, WIN), BF16),
            pltpu.VMEM((2 * edge, rows, WIN), BF16),
            dma((others,)), dma((others,)),
            dma((col_tiles - 1,)), dma((col_tiles - 1,)),
            dma((col_tiles,)), dma((2 * edge,)),
        ],
        compiler_params=pltpu.CompilerParams(collective_id=0, has_side_effects=True),
        name="field",
    )(shear, volume)
    tables = jnp.asarray(dft_tables())
    grads = pl.pallas_call(
        patch_kernel,
        out_shape=jax.ShapeDtypeStruct((slots, rows, WIN), BF16),
        in_specs=[smem, vmem, vmem, vmem, vmem],
        out_specs=vmem,
        scratch_shapes=[pltpu.VMEM((WIN // PATCH, slots * rows, PATCH), F32) for _ in range(3)],
        name="patches",
    )(positions[0, 0], ext, probe, measured[0, 0], tables)
    return pl.pallas_call(
        functools.partial(back_kernel, slabs, strips),
        out_shape=jax.ShapeDtypeStruct(volume.shape, BF16),
        in_specs=[smem, vmem],
        out_specs=vmem,
        scratch_shapes=[
            pltpu.VMEM((col_tiles - 1, rows, WIN), BF16),
            pltpu.VMEM((col_tiles, rows, WIN), BF16),
            pltpu.VMEM((rows, wide), F32),
            pltpu.VMEM((rows, wide), BF16),
            pltpu.VMEM((others, rows, wide), BF16),
            dma((others,)), dma((others,)),
            dma((col_tiles - 1,)), dma((col_tiles - 1,)),
            dma((2 * edge,)), dma((col_tiles,)),
        ],
        compiler_params=pltpu.CompilerParams(collective_id=1, has_side_effects=True),
        name="back",
    )(shear, grads)


def solution(mesh):
    placed = (
        P("slab", "strip", None),
        P(None, "slab"),
        P(),
        P("slab", "strip", None, None),
        P("slab", "strip", None, None, None),
    )
    return jax.shard_map(
        functools.partial(local, mesh.shape["slab"], mesh.shape["strip"]),
        mesh=mesh, in_specs=placed, out_specs=P("slab", "strip", None), check_vma=False,
    )
```

```python
import functools
import math

import jax
import jax.numpy as jnp
import numpy as np
from jax import lax
from jax.experimental import pallas as pl
from jax.experimental.pallas import tpu as pltpu
from jax.sharding import PartitionSpec as P

TILE_W = 128
PATCH = 128
RIM = PATCH // 2
WIN = TILE_W + 2 * RIM
GRAD_SCALE = 0.125
PAIRS = 4
MESH = pl.DeviceIdType.MESH
F32 = jnp.float32
BF16 = jnp.bfloat16


def dft_tables():
    index = np.arange(PATCH)
    angle = 2.0 * math.pi * ((index[:, None] * index[None, :]) % PATCH) / PATCH
    cosine = np.cos(angle) / math.sqrt(PATCH)
    sine = np.sin(angle) / math.sqrt(PATCH)
    first = np.block([[cosine, -sine], [sine, cosine]])
    out = []
    for table in (first, first.T):
        high = table.astype(BF16)
        out.append(high)
        out.append((table - high.astype(np.float64)).astype(BF16))
    return np.stack(out)


def place():
    slab = lax.axis_index("slab")
    strip = lax.axis_index("strip")
    return slab, strip


def greet(slab, strip, slabs, strips, col_tiles, edge):
    group, col = strip // col_tiles, strip % col_tiles
    groups = strips // col_tiles
    barrier = pltpu.get_barrier_semaphore()

    def signal(to_slab, to_strip):
        pl.semaphore_signal(
            barrier, inc=1, device_id={"slab": to_slab, "strip": to_strip}, device_id_type=MESH
        )

    for step in range(1, slabs):
        signal(lax.rem(slab + step, slabs), strip)
    for step in range(1, col_tiles):
        signal(slab, group * col_tiles + lax.rem(col + step, col_tiles))

    def greet_group(other, near, far_first):
        @pl.when(near)
        def _():
            for tile in range(col_tiles):
                signal(slab, other * col_tiles + tile)

        @pl.when(jnp.logical_not(near))
        def _():
            for tile in range(edge):
                signal(slab, other * col_tiles + far_first + tile)

    @pl.when(group > 0)
    def _():
        greet_group(group - 1, col < edge, col_tiles - edge)

    @pl.when(group < groups - 1)
    def _():
        greet_group(group + 1, col >= col_tiles - edge, 0)

    base = slabs - 1 + col_tiles - 1
    above = jnp.where(group > 0, jnp.where(col < edge, col_tiles, edge), 0)
    below = jnp.where(group < groups - 1, jnp.where(col >= col_tiles - edge, col_tiles, edge), 0)
    return barrier, base + above + below


def field_kernel(
    slabs, strips, shear_ref, vol_ref, ext_ref,
    part, slab_in, proj, land, land_edge,
    slab_send, slab_recv, send, recv, edge_send, edge_recv,
):
    depth, rows, width = vol_ref.shape
    wide = width + 2 * RIM
    col_tiles = width // TILE_W
    groups = strips // col_tiles
    edge = RIM // rows
    slab, strip = place()
    group, col = strip // col_tiles, strip % col_tiles
    barrier, peers = greet(slab, strip, slabs, strips, col_tiles, edge)
    lane = lax.broadcasted_iota(jnp.int32, (rows, wide), 1)
    inside = (lane >= RIM) & (lane < RIM + width)
    zeros = jnp.zeros((rows, 2 * RIM), F32)

    def partial(view):
        total = jnp.zeros((rows, wide), F32)
        for z in range(depth):
            layer = jnp.concatenate([vol_ref[z].astype(F32), zeros], 1)
            total = total + pltpu.roll(layer, shear_ref[view, z] + RIM, 1)
        return jnp.where(inside, total, 0.0).astype(BF16)

    copies = []
    for step in range(1, slabs):
        view = lax.rem(slab + step, slabs)
        part[step - 1] = partial(view)
        if step == 1:
            pl.semaphore_wait(barrier, peers)
        copy = pltpu.make_async_remote_copy(
            src_ref=part.at[step - 1], dst_ref=slab_in.at[step - 1],
            send_sem=slab_send.at[step - 1], recv_sem=slab_recv.at[step - 1],
            device_id={"slab": view, "strip": strip}, device_id_type=MESH,
        )
        copy.start()
        copies.append(copy)
    total = partial(slab).astype(F32)
    if slabs == 1:
        pl.semaphore_wait(barrier, peers)
    for step in range(1, slabs):
        copies[step - 1].wait_recv()
        total = total + slab_in[step - 1].astype(F32)
    proj[...] = total.astype(BF16)

    def window(tile):
        return pl.ds(pl.multiple_of(tile * TILE_W, TILE_W), WIN)

    top = (col < edge) & (group > 0)
    bottom = (col >= col_tiles - edge) & (group < groups - 1)
    other = jnp.where(col < edge, group - 1, group + 1)
    slot = jnp.where(col < edge, edge + col, col - (col_tiles - edge))

    def edge_copy(tile):
        return pltpu.make_async_remote_copy(
            src_ref=proj.at[:, pl.ds(tile * TILE_W, WIN)], dst_ref=land_edge.at[slot],
            send_sem=edge_send.at[tile], recv_sem=edge_recv.at[slot],
            device_id={"slab": slab, "strip": other * col_tiles + tile}, device_id_type=MESH,
        )

    @pl.when(top | bottom)
    def _():
        for tile in range(col_tiles):
            edge_copy(tile).start()

    group_copies = []
    for step in range(1, col_tiles):
        tile = lax.rem(col + step, col_tiles)
        copy = pltpu.make_async_remote_copy(
            src_ref=proj.at[:, window(tile)], dst_ref=land.at[step - 1],
            send_sem=send.at[step - 1], recv_sem=recv.at[step - 1],
            device_id={"slab": slab, "strip": group * col_tiles + tile}, device_id_type=MESH,
        )
        copy.start()
        group_copies.append(copy)
    ext_ref[edge + col] = proj[:, window(col)]
    for step in range(1, col_tiles):
        group_copies[step - 1].wait_recv()
        ext_ref[edge + lax.rem(col + col_tiles - step, col_tiles)] = land[step - 1]

    def edge_in(first, place_at, has):
        @pl.when(has)
        def _():
            for k in range(edge):
                pltpu.make_async_remote_copy(
                    src_ref=proj.at[:, pl.ds(0, WIN)], dst_ref=land_edge.at[first + k],
                    send_sem=edge_send.at[0], recv_sem=edge_recv.at[first + k],
                    device_id={"slab": slab, "strip": other * col_tiles}, device_id_type=MESH,
                ).wait_recv()
                ext_ref[place_at + k] = land_edge[first + k]

        @pl.when(jnp.logical_not(has))
        def _():
            for k in range(edge):
                ext_ref[place_at + k] = jnp.zeros((rows, WIN), BF16)

    edge_in(0, 0, group > 0)
    edge_in(edge, edge + col_tiles, group < groups - 1)
    for copy in copies:
        copy.wait_send()
    for copy in group_copies:
        copy.wait_send()

    @pl.when(top | bottom)
    def _():
        for tile in range(col_tiles):
            edge_copy(tile).wait_send()


def cos_sin(x):
    turn = jnp.floor(x * (2.0 / math.pi) + 0.5)
    r = ((x - turn * 1.5703125) - turn * 4.837512969970703125e-4) - turn * 7.54978995489188216e-8
    z = r * r
    s = ((-1.9515295891e-4 * z + 8.3321608736e-3) * z - 1.6666654611e-1) * z * r + r
    c = ((2.443315711809948e-5 * z - 1.388731625493765e-3) * z + 4.166664568298827e-2) * z * z
    c = c - 0.5 * z + 1.0
    quarter = turn.astype(jnp.int32) & 3
    odd = (quarter & 1) == 1
    cos = jnp.where(odd, s, c)
    sin = jnp.where(odd, c, s)
    cos = jnp.where((quarter == 1) | (quarter == 2), -cos, cos)
    sin = jnp.where(quarter >= 2, -sin, sin)
    return cos, sin


def split(x):
    high = x.astype(BF16)
    return high, (x - high.astype(F32)).astype(BF16)


def mm(a, b):
    return jnp.dot(a, b, preferred_element_type=F32)


def patch_kernel(pos_ref, ext_ref, probe_ref, meas_ref, tab_ref, out_ref, cosf, sinf, acc):
    slots, rows, _ = ext_ref.shape
    count = meas_ref.shape[0]
    halves = WIN // PATCH

    def right(x, which):
        return mm(x.astype(BF16), tab_ref[2 * which])

    def left(which, x):
        return mm(tab_ref[2 * which], x.astype(BF16))

    def right3(x, which):
        high, low = split(x)
        t_high, t_low = tab_ref[2 * which], tab_ref[2 * which + 1]
        return mm(high, t_high) + (mm(low, t_high) + mm(high, t_low))

    def left3(which, x):
        high, low = split(x)
        t_high, t_low = tab_ref[2 * which], tab_ref[2 * which + 1]
        return mm(t_high, high) + (mm(t_high, low) + mm(t_low, high))

    def regroup(x):
        return jnp.concatenate(
            [
                jnp.concatenate([x[:PATCH, :PATCH], x[PATCH:, :PATCH]], 1),
                jnp.concatenate([x[:PATCH, PATCH:], x[PATCH:, PATCH:]], 1),
            ],
            0,
        )

    def trig(j, _):
        cos, sin = cos_sin(ext_ref[j].astype(F32))
        at = pl.ds(pl.multiple_of(j * rows, rows), rows)
        for h in range(halves):
            cosf[h, at, :] = cos[:, h * PATCH : (h + 1) * PATCH]
            sinf[h, at, :] = sin[:, h * PATCH : (h + 1) * PATCH]
            acc[h, at, :] = jnp.zeros((rows, PATCH), F32)
        return 0

    lax.fori_loop(0, slots, trig, 0, unroll=2)

    def cut(field, row, by):
        strips = [field[h, pl.ds(row, PATCH), :] for h in range(halves)]
        return pltpu.roll(jnp.concatenate(strips, 1), by, 1)[:, :PATCH]

    def pairs(j, _):
        probe_re, probe_im = probe_ref[0], probe_ref[1]
        members = [PAIRS * j + u for u in range(PAIRS)]
        where, cuts, halves_in = [], [], []
        for i in members:
            waves = []
            for k in range(2):
                row = pos_ref[0, 2 * i + k] + RIM
                lane = pos_ref[1, 2 * i + k] + RIM
                back_by = (WIN - lane) & (WIN - 1)
                cos = cut(cosf, row, back_by)
                sin = cut(sinf, row, back_by)
                where.append((row, lane))
                cuts.append((cos, sin))
                wave_re = probe_re * cos - probe_im * sin
                wave_im = probe_re * sin + probe_im * cos
                waves.append(jnp.concatenate([wave_re, wave_im], 1))
            halves_in.append(jnp.concatenate(waves, 0))
        half = [regroup(right3(x, 0)) for x in halves_in]
        far = [left3(1, x) for x in half]
        weighted = []
        for i, x in zip(members, far):
            far_re, far_im = x[:PATCH], x[PATCH:]
            meas = jnp.concatenate([meas_ref[2 * i], meas_ref[2 * i + 1]], 1).astype(F32)
            weight = GRAD_SCALE * (far_re * far_re + far_im * far_im - meas)
            weighted.append(jnp.concatenate([weight * far_re, weight * far_im], 0))
        half = [regroup(left(0, x)) for x in weighted]
        back = [right(x, 1) for x in half]
        for u in range(2 * PAIRS):
            row, lane = where[u]
            cos, sin = cuts[u]
            k = u % 2
            back_re = back[u // 2][k * PATCH : (k + 1) * PATCH, :PATCH]
            back_im = back[u // 2][k * PATCH : (k + 1) * PATCH, PATCH:]
            grad_re = probe_re * back_re + probe_im * back_im
            grad_im = probe_re * back_im - probe_im * back_re
            grad = cos * grad_im - sin * grad_re
            grad = jnp.concatenate([grad, jnp.zeros_like(grad)], 1)
            at = pl.ds(row, PATCH)
            grad = pltpu.roll(grad, lane, 1)
            for h in range(halves):
                acc[h, at, :] = acc[h, at, :] + grad[:, h * PATCH : (h + 1) * PATCH]
        return 0

    lax.fori_loop(0, count // (2 * PAIRS), pairs, 0)

    def finish(j, _):
        at = pl.ds(pl.multiple_of(j * rows, rows), rows)
        out_ref[j] = jnp.concatenate([acc[h, at, :] for h in range(halves)], 1).astype(BF16)
        return 0

    lax.fori_loop(0, slots, finish, 0)


def back_kernel(
    slabs, strips, grad_ref, out_ref,
    land, land_edge, total, own, slab_in,
    slab_send, slab_recv, send, recv, edge_send, edge_recv,
):
    _, rows, wide = out_ref.shape
    width = wide - 2 * RIM
    col_tiles = width // TILE_W
    groups = strips // col_tiles
    edge = RIM // rows
    slab, strip = place()
    group, col = strip // col_tiles, strip % col_tiles
    barrier, peers = greet(slab, strip, slabs, strips, col_tiles, edge)
    pl.semaphore_wait(barrier, peers)

    def edge_copy(k, other, source, owner):
        return pltpu.make_async_remote_copy(
            src_ref=grad_ref.at[source], dst_ref=land_edge.at[col],
            send_sem=edge_send.at[k], recv_sem=edge_recv.at[col],
            device_id={"slab": slab, "strip": other * col_tiles + owner}, device_id_type=MESH,
        )

    def edge_copies(act):
        @pl.when(group > 0)
        def _():
            for k in range(edge):
                act(edge_copy(k, group - 1, k, col_tiles - edge + k))

        @pl.when(group < groups - 1)
        def _():
            for k in range(edge):
                act(edge_copy(edge + k, group + 1, edge + col_tiles + k, k))

    edge_copies(lambda copy: copy.start())
    group_copies = []
    for step in range(1, col_tiles):
        tile = lax.rem(col + step, col_tiles)
        copy = pltpu.make_async_remote_copy(
            src_ref=grad_ref.at[edge + tile], dst_ref=land.at[step - 1],
            send_sem=send.at[step - 1], recv_sem=recv.at[step - 1],
            device_id={"slab": slab, "strip": group * col_tiles + tile}, device_id_type=MESH,
        )
        copy.start()
        group_copies.append(copy)
    total[...] = jnp.zeros((rows, wide), F32)

    def window(tile):
        return pl.ds(pl.multiple_of(tile * TILE_W, TILE_W), WIN)

    total[:, window(col)] = total[:, window(col)] + grad_ref[edge + col].astype(F32)
    for step in range(1, col_tiles):
        group_copies[step - 1].wait_recv()
        at = window(lax.rem(col + col_tiles - step, col_tiles))
        total[:, at] = total[:, at] + land[step - 1].astype(F32)

    has_edge = ((col < edge) & (group > 0)) | ((col >= col_tiles - edge) & (group < groups - 1))
    other = jnp.where(col < edge, group - 1, group + 1)

    @pl.when(has_edge)
    def _():
        for tile in range(col_tiles):
            pltpu.make_async_remote_copy(
                src_ref=grad_ref.at[0], dst_ref=land_edge.at[tile],
                send_sem=edge_send.at[0], recv_sem=edge_recv.at[tile],
                device_id={"slab": slab, "strip": other * col_tiles + tile}, device_id_type=MESH,
            ).wait_recv()
            at = window(tile)
            total[:, at] = total[:, at] + land_edge[tile].astype(F32)

    lane = lax.broadcasted_iota(jnp.int32, (rows, wide), 1)
    inside = (lane >= RIM) & (lane < RIM + width)
    mine = jnp.where(inside, total[...], 0.0).astype(BF16)
    own[...] = mine
    copies = []
    for step in range(1, slabs):
        copy = pltpu.make_async_remote_copy(
            src_ref=own, dst_ref=slab_in.at[step - 1],
            send_sem=slab_send.at[step - 1], recv_sem=slab_recv.at[step - 1],
            device_id={"slab": lax.rem(slab + step, slabs), "strip": strip}, device_id_type=MESH,
        )
        copy.start()
        copies.append(copy)

    out_ref[slab] = mine
    for step in range(1, slabs):
        copies[step - 1].wait_recv()
        out_ref[lax.rem(slab + slabs - step, slabs)] = slab_in[step - 1]
    for copy in copies:
        copy.wait_send()
    for copy in group_copies:
        copy.wait_send()
    edge_copies(lambda copy: copy.wait_send())


def spread_kernel(shear_ref, fields_ref, out_ref):
    depth, rows, width = out_ref.shape
    views, _, wide = fields_ref.shape
    for z in range(depth):
        result = jnp.zeros((rows, width), F32)
        for view in range(views):
            by = lax.rem(wide - RIM - shear_ref[view, z], wide)
            result = result + pltpu.roll(fields_ref[view].astype(F32), by, 1)[:, :width]
        out_ref[z] = result.astype(BF16)


def local(slabs, strips, volume, shear, probe, positions, measured):
    depth, rows, width = volume.shape
    col_tiles = width // TILE_W
    wide = width + 2 * RIM
    edge = RIM // rows
    slots = col_tiles + 2 * edge
    others = max(slabs - 1, 1)
    vmem = pl.BlockSpec(memory_space=pltpu.VMEM)
    smem = pl.BlockSpec(memory_space=pltpu.SMEM)
    dma = pltpu.SemaphoreType.DMA
    ext = pl.pallas_call(
        functools.partial(field_kernel, slabs, strips),
        out_shape=jax.ShapeDtypeStruct((slots, rows, WIN), BF16),
        in_specs=[smem, vmem],
        out_specs=vmem,
        scratch_shapes=[
            pltpu.VMEM((others, rows, wide), BF16),
            pltpu.VMEM((others, rows, wide), BF16),
            pltpu.VMEM((rows, wide), BF16),
            pltpu.VMEM((col_tiles - 1, rows, WIN), BF16),
            pltpu.VMEM((2 * edge, rows, WIN), BF16),
            dma((others,)), dma((others,)),
            dma((col_tiles - 1,)), dma((col_tiles - 1,)),
            dma((col_tiles,)), dma((2 * edge,)),
        ],
        compiler_params=pltpu.CompilerParams(collective_id=0, has_side_effects=True),
        name="field",
    )(shear, volume)
    tables = jnp.asarray(dft_tables())
    grads = pl.pallas_call(
        patch_kernel,
        out_shape=jax.ShapeDtypeStruct((slots, rows, WIN), BF16),
        in_specs=[smem, vmem, vmem, vmem, vmem],
        out_specs=vmem,
        scratch_shapes=[pltpu.VMEM((WIN // PATCH, slots * rows, PATCH), F32) for _ in range(3)],
        name="patches",
    )(positions[0, 0].T, ext, probe, measured[0, 0], tables)
    fields = pl.pallas_call(
        functools.partial(back_kernel, slabs, strips),
        out_shape=jax.ShapeDtypeStruct((slabs, rows, wide), BF16),
        in_specs=[vmem],
        out_specs=vmem,
        scratch_shapes=[
            pltpu.VMEM((col_tiles - 1, rows, WIN), BF16),
            pltpu.VMEM((col_tiles, rows, WIN), BF16),
            pltpu.VMEM((rows, wide), F32),
            pltpu.VMEM((rows, wide), BF16),
            pltpu.VMEM((others, rows, wide), BF16),
            dma((others,)), dma((others,)),
            dma((col_tiles - 1,)), dma((col_tiles - 1,)),
            dma((2 * edge,)), dma((col_tiles,)),
        ],
        compiler_params=pltpu.CompilerParams(collective_id=1, has_side_effects=True),
        name="back",
    )(grads)
    return pl.pallas_call(
        spread_kernel,
        out_shape=jax.ShapeDtypeStruct(volume.shape, BF16),
        in_specs=[smem, vmem],
        out_specs=vmem,
        name="spread",
    )(shear, fields)


def solution(mesh):
    placed = (
        P("slab", "strip", None),
        P(None, "slab"),
        P(),
        P("slab", "strip", None, None),
        P("slab", "strip", None, None, None),
    )
    return jax.shard_map(
        functools.partial(local, mesh.shape["slab"], mesh.shape["strip"]),
        mesh=mesh, in_specs=placed, out_specs=P("slab", "strip", None), check_vma=False,
    )
```

```python
import functools
import math

import jax
import jax.numpy as jnp
import numpy as np
from jax import lax
from jax.experimental import pallas as pl
from jax.experimental.pallas import tpu as pltpu
from jax.sharding import PartitionSpec as P

TILE_W = 128
PATCH = 128
RIM = PATCH // 2
WIN = TILE_W + 2 * RIM
GRAD_SCALE = 0.125
PAIRS = 4
MESH = pl.DeviceIdType.MESH
F32 = jnp.float32
BF16 = jnp.bfloat16


def dft_tables():
    index = np.arange(PATCH)
    angle = 2.0 * math.pi * ((index[:, None] * index[None, :]) % PATCH) / PATCH
    cosine = np.cos(angle) / math.sqrt(PATCH)
    sine = np.sin(angle) / math.sqrt(PATCH)
    first = np.block([[cosine, -sine], [sine, cosine]])
    out = []
    for table in (first, first.T):
        high = table.astype(BF16)
        out.append(high)
        out.append((table - high.astype(np.float64)).astype(BF16))
    return np.stack(out)


def place():
    slab = lax.axis_index("slab")
    strip = lax.axis_index("strip")
    return slab, strip


def greet(slab, strip, slabs, strips, col_tiles, edge):
    group, col = strip // col_tiles, strip % col_tiles
    groups = strips // col_tiles
    barrier = pltpu.get_barrier_semaphore()

    def signal(to_slab, to_strip):
        pl.semaphore_signal(
            barrier, inc=1, device_id={"slab": to_slab, "strip": to_strip}, device_id_type=MESH
        )

    for step in range(1, slabs):
        signal(lax.rem(slab + step, slabs), strip)
    for step in range(1, col_tiles):
        signal(slab, group * col_tiles + lax.rem(col + step, col_tiles))

    def greet_group(other, near, far_first):
        @pl.when(near)
        def _():
            for tile in range(col_tiles):
                signal(slab, other * col_tiles + tile)

        @pl.when(jnp.logical_not(near))
        def _():
            for tile in range(edge):
                signal(slab, other * col_tiles + far_first + tile)

    @pl.when(group > 0)
    def _():
        greet_group(group - 1, col < edge, col_tiles - edge)

    @pl.when(group < groups - 1)
    def _():
        greet_group(group + 1, col >= col_tiles - edge, 0)

    base = slabs - 1 + col_tiles - 1
    above = jnp.where(group > 0, jnp.where(col < edge, col_tiles, edge), 0)
    below = jnp.where(group < groups - 1, jnp.where(col >= col_tiles - edge, col_tiles, edge), 0)
    return barrier, base + above + below


def cos_sin(x):
    turn = jnp.floor(x * (2.0 / math.pi) + 0.5)
    r = ((x - turn * 1.5703125) - turn * 4.837512969970703125e-4) - turn * 7.54978995489188216e-8
    z = r * r
    s = ((-1.9515295891e-4 * z + 8.3321608736e-3) * z - 1.6666654611e-1) * z * r + r
    c = ((2.443315711809948e-5 * z - 1.388731625493765e-3) * z + 4.166664568298827e-2) * z * z
    c = c - 0.5 * z + 1.0
    quarter = turn.astype(jnp.int32) & 3
    odd = (quarter & 1) == 1
    cos = jnp.where(odd, s, c)
    sin = jnp.where(odd, c, s)
    cos = jnp.where((quarter == 1) | (quarter == 2), -cos, cos)
    sin = jnp.where(quarter >= 2, -sin, sin)
    return cos, sin


def split(x):
    high = x.astype(BF16)
    return high, (x - high.astype(F32)).astype(BF16)


def mm(a, b):
    return jnp.dot(a, b, preferred_element_type=F32)


def grad_kernel(
    slabs, strips, shear_ref, pos_ref, vol_ref, probe_any, meas_any, tab_any, out_ref,
    probe_ref, meas_ref, tab_ref, load_sem,
    part, slab_in, proj, land, land_edge,
    cosf, sinf, acc, grad_ref, grad_land, grad_edge, total, own, grad_slab,
    slab_send, slab_recv, send, recv, edge_send, edge_recv,
    b_slab_send, b_slab_recv, b_send, b_recv, b_edge_send, b_edge_recv,
):
    pairs_of = ((probe_any, probe_ref), (meas_any, meas_ref), (tab_any, tab_ref))
    loads = [pltpu.make_async_copy(a, b, load_sem.at[k]) for k, (a, b) in enumerate(pairs_of)]
    for load in loads:
        load.start()
    depth, rows, width = vol_ref.shape
    wide = width + 2 * RIM
    col_tiles = width // TILE_W
    groups = strips // col_tiles
    edge = RIM // rows
    slots = col_tiles + 2 * edge
    halves = WIN // PATCH
    slab, strip = place()
    group, col = strip // col_tiles, strip % col_tiles
    barrier, peers = greet(slab, strip, slabs, strips, col_tiles, edge)
    lane = lax.broadcasted_iota(jnp.int32, (rows, wide), 1)
    inside = (lane >= RIM) & (lane < RIM + width)
    zeros = jnp.zeros((rows, 2 * RIM), F32)

    def put(field, at, value):
        for h in range(halves):
            field[h, at, :] = value[:, h * PATCH : (h + 1) * PATCH]

    def trig(place_at, phase):
        cos, sin = cos_sin(phase.astype(F32))
        at = pl.ds(pl.multiple_of(place_at * rows, rows), rows)
        put(cosf, at, cos)
        put(sinf, at, sin)

    def partial(view):
        total = jnp.zeros((rows, wide), F32)
        for z in range(depth):
            layer = jnp.concatenate([vol_ref[z].astype(F32), zeros], 1)
            total = total + pltpu.roll(layer, shear_ref[view, z] + RIM, 1)
        return jnp.where(inside, total, 0.0).astype(BF16)

    copies = []
    for step in range(1, slabs):
        view = lax.rem(slab + step, slabs)
        part[step - 1] = partial(view)
        if step == 1:
            pl.semaphore_wait(barrier, peers)
        copy = pltpu.make_async_remote_copy(
            src_ref=part.at[step - 1], dst_ref=slab_in.at[step - 1],
            send_sem=slab_send.at[step - 1], recv_sem=slab_recv.at[step - 1],
            device_id={"slab": view, "strip": strip}, device_id_type=MESH,
        )
        copy.start()
        copies.append(copy)
    summed = partial(slab).astype(F32)
    if slabs == 1:
        pl.semaphore_wait(barrier, peers)
    for step in range(1, slabs):
        copies[step - 1].wait_recv()
        summed = summed + slab_in[step - 1].astype(F32)
    proj[...] = summed.astype(BF16)

    def window(tile):
        return pl.ds(pl.multiple_of(tile * TILE_W, TILE_W), WIN)

    top = (col < edge) & (group > 0)
    bottom = (col >= col_tiles - edge) & (group < groups - 1)
    other = jnp.where(col < edge, group - 1, group + 1)
    slot = jnp.where(col < edge, edge + col, col - (col_tiles - edge))

    def edge_copy(tile):
        return pltpu.make_async_remote_copy(
            src_ref=proj.at[:, pl.ds(tile * TILE_W, WIN)], dst_ref=land_edge.at[slot],
            send_sem=edge_send.at[tile], recv_sem=edge_recv.at[slot],
            device_id={"slab": slab, "strip": other * col_tiles + tile}, device_id_type=MESH,
        )

    @pl.when(top | bottom)
    def _():
        for tile in range(col_tiles):
            edge_copy(tile).start()

    group_copies = []
    for step in range(1, col_tiles):
        tile = lax.rem(col + step, col_tiles)
        copy = pltpu.make_async_remote_copy(
            src_ref=proj.at[:, window(tile)], dst_ref=land.at[step - 1],
            send_sem=send.at[step - 1], recv_sem=recv.at[step - 1],
            device_id={"slab": slab, "strip": group * col_tiles + tile}, device_id_type=MESH,
        )
        copy.start()
        group_copies.append(copy)
    trig(edge + col, proj[:, window(col)])
    acc[...] = jnp.zeros_like(acc)
    for step in range(1, col_tiles):
        group_copies[step - 1].wait_recv()
        trig(edge + lax.rem(col + col_tiles - step, col_tiles), land[step - 1])

    def edge_in(first, place_at, has):
        @pl.when(has)
        def _():
            for k in range(edge):
                pltpu.make_async_remote_copy(
                    src_ref=proj.at[:, pl.ds(0, WIN)], dst_ref=land_edge.at[first + k],
                    send_sem=edge_send.at[0], recv_sem=edge_recv.at[first + k],
                    device_id={"slab": slab, "strip": other * col_tiles}, device_id_type=MESH,
                ).wait_recv()
                trig(place_at + k, land_edge[first + k])

        @pl.when(jnp.logical_not(has))
        def _():
            for k in range(edge):
                at = pl.ds((place_at + k) * rows, rows)
                put(cosf, at, jnp.ones((rows, WIN), F32))
                put(sinf, at, jnp.zeros((rows, WIN), F32))

    edge_in(0, 0, group > 0)
    edge_in(edge, edge + col_tiles, group < groups - 1)

    for load in loads:
        load.wait()
    count = meas_ref.shape[0]

    def right(x, which):
        return mm(x.astype(BF16), tab_ref[2 * which])

    def left(which, x):
        return mm(tab_ref[2 * which], x.astype(BF16))

    def right3(x, which):
        high, low = split(x)
        t_high, t_low = tab_ref[2 * which], tab_ref[2 * which + 1]
        return mm(high, t_high) + (mm(low, t_high) + mm(high, t_low))

    def left3(which, x):
        high, low = split(x)
        t_high, t_low = tab_ref[2 * which], tab_ref[2 * which + 1]
        return mm(t_high, high) + (mm(t_high, low) + mm(t_low, high))

    def regroup(x):
        return jnp.concatenate(
            [
                jnp.concatenate([x[:PATCH, :PATCH], x[PATCH:, :PATCH]], 1),
                jnp.concatenate([x[:PATCH, PATCH:], x[PATCH:, PATCH:]], 1),
            ],
            0,
        )

    def cut(field, row, by):
        strips = [field[h, pl.ds(row, PATCH), :] for h in range(halves)]
        return pltpu.roll(jnp.concatenate(strips, 1), by, 1)[:, :PATCH]

    def pairs(j, _):
        probe_re, probe_im = probe_ref[0], probe_ref[1]
        members = [PAIRS * j + u for u in range(PAIRS)]
        where, cuts, halves_in = [], [], []
        for i in members:
            waves = []
            for k in range(2):
                row = pos_ref[0, 2 * i + k] + RIM
                lane = pos_ref[1, 2 * i + k] + RIM
                back_by = (WIN - lane) & (WIN - 1)
                cos = cut(cosf, row, back_by)
                sin = cut(sinf, row, back_by)
                where.append((row, lane))
                cuts.append((cos, sin))
                wave_re = probe_re * cos - probe_im * sin
                wave_im = probe_re * sin + probe_im * cos
                waves.append(jnp.concatenate([wave_re, wave_im], 1))
            halves_in.append(jnp.concatenate(waves, 0))
        half = [regroup(right3(x, 0)) for x in halves_in]
        far = [left3(1, x) for x in half]
        weighted = []
        for i, x in zip(members, far):
            far_re, far_im = x[:PATCH], x[PATCH:]
            meas = jnp.concatenate([meas_ref[2 * i], meas_ref[2 * i + 1]], 1).astype(F32)
            weight = GRAD_SCALE * (far_re * far_re + far_im * far_im - meas)
            weighted.append(jnp.concatenate([weight * far_re, weight * far_im], 0))
        half = [regroup(left(0, x)) for x in weighted]
        back = [right(x, 1) for x in half]
        placed, rows_at = [], []
        for u in range(2 * PAIRS):
            row, lane = where[u]
            cos, sin = cuts[u]
            k = u % 2
            back_re = back[u // 2][k * PATCH : (k + 1) * PATCH, :PATCH]
            back_im = back[u // 2][k * PATCH : (k + 1) * PATCH, PATCH:]
            grad_re = probe_re * back_re + probe_im * back_im
            grad_im = probe_re * back_im - probe_im * back_re
            grad = cos * grad_im - sin * grad_re
            grad = jnp.concatenate([grad, jnp.zeros_like(grad)], 1)
            placed.append(pltpu.roll(grad, lane, 1).astype(BF16))
            rows_at.append(lax.broadcasted_iota(jnp.int32, (1, PATCH), 1) + row)
        row_at = jnp.concatenate(rows_at, 1)
        ext_row = lax.broadcasted_iota(jnp.int32, (slots * rows, row_at.shape[1]), 0)
        select = jnp.where(ext_row == row_at, 1.0, 0.0).astype(BF16)
        acc[...] = acc[...] + mm(select, jnp.concatenate(placed, 0))
        return 0

    lax.fori_loop(0, count // (2 * PAIRS), pairs, 0)

    grad_ref[...] = acc[...].astype(BF16).reshape(slots, rows, WIN)

    def b_edge_copy(k, other, source, owner):
        return pltpu.make_async_remote_copy(
            src_ref=grad_ref.at[source], dst_ref=grad_edge.at[col],
            send_sem=b_edge_send.at[k], recv_sem=b_edge_recv.at[col],
            device_id={"slab": slab, "strip": other * col_tiles + owner}, device_id_type=MESH,
        )

    def b_edge_copies(act):
        @pl.when(group > 0)
        def _():
            for k in range(edge):
                act(b_edge_copy(k, group - 1, k, col_tiles - edge + k))

        @pl.when(group < groups - 1)
        def _():
            for k in range(edge):
                act(b_edge_copy(edge + k, group + 1, edge + col_tiles + k, k))

    b_edge_copies(lambda copy: copy.start())
    b_group_copies = []
    for step in range(1, col_tiles):
        tile = lax.rem(col + step, col_tiles)
        copy = pltpu.make_async_remote_copy(
            src_ref=grad_ref.at[edge + tile], dst_ref=grad_land.at[step - 1],
            send_sem=b_send.at[step - 1], recv_sem=b_recv.at[step - 1],
            device_id={"slab": slab, "strip": group * col_tiles + tile}, device_id_type=MESH,
        )
        copy.start()
        b_group_copies.append(copy)
    total[...] = jnp.zeros((rows, wide), F32)

    total[:, window(col)] = total[:, window(col)] + grad_ref[edge + col].astype(F32)
    for step in range(1, col_tiles):
        b_group_copies[step - 1].wait_recv()
        at = window(lax.rem(col + col_tiles - step, col_tiles))
        total[:, at] = total[:, at] + grad_land[step - 1].astype(F32)

    has_edge = ((col < edge) & (group > 0)) | ((col >= col_tiles - edge) & (group < groups - 1))
    other = jnp.where(col < edge, group - 1, group + 1)

    @pl.when(has_edge)
    def _():
        for tile in range(col_tiles):
            pltpu.make_async_remote_copy(
                src_ref=grad_ref.at[0], dst_ref=grad_edge.at[tile],
                send_sem=b_edge_send.at[0], recv_sem=b_edge_recv.at[tile],
                device_id={"slab": slab, "strip": other * col_tiles + tile}, device_id_type=MESH,
            ).wait_recv()
            at = window(tile)
            total[:, at] = total[:, at] + grad_edge[tile].astype(F32)

    mine = jnp.where(inside, total[...], 0.0).astype(BF16)
    own[...] = mine
    b_copies = []
    for step in range(1, slabs):
        copy = pltpu.make_async_remote_copy(
            src_ref=own, dst_ref=grad_slab.at[step - 1],
            send_sem=b_slab_send.at[step - 1], recv_sem=b_slab_recv.at[step - 1],
            device_id={"slab": lax.rem(slab + step, slabs), "strip": strip}, device_id_type=MESH,
        )
        copy.start()
        b_copies.append(copy)

    out_ref[slab] = mine
    for step in range(1, slabs):
        b_copies[step - 1].wait_recv()
        out_ref[lax.rem(slab + slabs - step, slabs)] = grad_slab[step - 1]
    for copy in b_copies:
        copy.wait_send()
    for copy in b_group_copies:
        copy.wait_send()
    b_edge_copies(lambda copy: copy.wait_send())
    for copy in copies:
        copy.wait_send()
    for copy in group_copies:
        copy.wait_send()

    @pl.when(top | bottom)
    def _():
        for tile in range(col_tiles):
            edge_copy(tile).wait_send()


def spread_kernel(shear_ref, fields_ref, out_ref):
    depth, rows, width = out_ref.shape
    views, _, wide = fields_ref.shape
    for z in range(depth):
        result = jnp.zeros((rows, width), F32)
        for view in range(views):
            by = lax.rem(wide - RIM - shear_ref[view, z], wide)
            result = result + pltpu.roll(fields_ref[view].astype(F32), by, 1)[:, :width]
        out_ref[z] = result.astype(BF16)


def local(slabs, strips, volume, shear, probe, positions, measured):
    _, rows, width = volume.shape
    col_tiles = width // TILE_W
    wide = width + 2 * RIM
    edge = RIM // rows
    slots = col_tiles + 2 * edge
    others = max(slabs - 1, 1)
    vmem = pl.BlockSpec(memory_space=pltpu.VMEM)
    smem = pl.BlockSpec(memory_space=pltpu.SMEM)
    anywhere = pl.BlockSpec(memory_space=pl.ANY)
    dma = pltpu.SemaphoreType.DMA
    tables = jnp.asarray(dft_tables())
    patches = measured[0, 0]
    fields = pl.pallas_call(
        functools.partial(grad_kernel, slabs, strips),
        out_shape=jax.ShapeDtypeStruct((slabs, rows, wide), BF16),
        in_specs=[smem, smem, vmem, anywhere, anywhere, anywhere],
        out_specs=vmem,
        scratch_shapes=[
            pltpu.VMEM(probe.shape, F32),
            pltpu.VMEM(patches.shape, BF16),
            pltpu.VMEM(tables.shape, BF16),
            dma((3,)),
            pltpu.VMEM((others, rows, wide), BF16),
            pltpu.VMEM((others, rows, wide), BF16),
            pltpu.VMEM((rows, wide), BF16),
            pltpu.VMEM((col_tiles - 1, rows, WIN), BF16),
            pltpu.VMEM((2 * edge, rows, WIN), BF16),
            pltpu.VMEM((WIN // PATCH, slots * rows, PATCH), F32),
            pltpu.VMEM((WIN // PATCH, slots * rows, PATCH), F32),
            pltpu.VMEM((slots * rows, WIN), F32),
            pltpu.VMEM((slots, rows, WIN), BF16),
            pltpu.VMEM((col_tiles - 1, rows, WIN), BF16),
            pltpu.VMEM((col_tiles, rows, WIN), BF16),
            pltpu.VMEM((rows, wide), F32),
            pltpu.VMEM((rows, wide), BF16),
            pltpu.VMEM((others, rows, wide), BF16),
            dma((others,)), dma((others,)),
            dma((col_tiles - 1,)), dma((col_tiles - 1,)),
            dma((col_tiles,)), dma((2 * edge,)),
            dma((others,)), dma((others,)),
            dma((col_tiles - 1,)), dma((col_tiles - 1,)),
            dma((2 * edge,)), dma((col_tiles,)),
        ],
        compiler_params=pltpu.CompilerParams(collective_id=0, has_side_effects=True),
        name="gradient",
    )(shear, positions[0, 0].T, volume, probe, patches, tables)
    return pl.pallas_call(
        spread_kernel,
        out_shape=jax.ShapeDtypeStruct(volume.shape, BF16),
        in_specs=[smem, vmem],
        out_specs=vmem,
        name="spread",
    )(shear, fields)


def solution(mesh):
    placed = (
        P("slab", "strip", None),
        P(None, "slab"),
        P(),
        P("slab", "strip", None, None),
        P("slab", "strip", None, None, None),
    )
    return jax.shard_map(
        functools.partial(local, mesh.shape["slab"], mesh.shape["strip"]),
        mesh=mesh, in_specs=placed, out_specs=P("slab", "strip", None), check_vma=False,
    )
```

```python
import functools
import math

import jax
import jax.numpy as jnp
import numpy as np
from jax import lax
from jax.experimental import pallas as pl
from jax.experimental.pallas import tpu as pltpu
from jax.sharding import PartitionSpec as P

TILE_W = 128
PATCH = 128
RIM = PATCH // 2
WIN = TILE_W + 2 * RIM
GRAD_SCALE = 0.125
PAIRS = 8
CUTS = 1
MESH = pl.DeviceIdType.MESH
F32 = jnp.float32
BF16 = jnp.bfloat16


def dft_tables():
    index = np.arange(PATCH)
    angle = 2.0 * math.pi * ((index[:, None] * index[None, :]) % PATCH) / PATCH
    cosine = np.cos(angle) / math.sqrt(PATCH)
    sine = np.sin(angle) / math.sqrt(PATCH)
    first = np.block([[cosine, -sine], [sine, cosine]])
    out = []
    for table in (first, first.T):
        high = table.astype(BF16)
        out.append(high)
        out.append((table - high.astype(np.float64)).astype(BF16))
    return np.stack(out)


def place():
    slab = lax.axis_index("slab")
    strip = lax.axis_index("strip")
    return slab, strip


def greet(slab, strip, slabs, strips, col_tiles, edge):
    group, col = strip // col_tiles, strip % col_tiles
    groups = strips // col_tiles
    barrier = pltpu.get_barrier_semaphore()

    def signal(to_slab, to_strip):
        pl.semaphore_signal(
            barrier, inc=1, device_id={"slab": to_slab, "strip": to_strip}, device_id_type=MESH
        )

    for step in range(1, slabs):
        signal(lax.rem(slab + step, slabs), strip)
    for step in range(1, col_tiles):
        signal(slab, group * col_tiles + lax.rem(col + step, col_tiles))

    def greet_group(other, near, far_first):
        @pl.when(near)
        def _():
            for tile in range(col_tiles):
                signal(slab, other * col_tiles + tile)

        @pl.when(jnp.logical_not(near))
        def _():
            for tile in range(edge):
                signal(slab, other * col_tiles + far_first + tile)

    @pl.when(group > 0)
    def _():
        greet_group(group - 1, col < edge, col_tiles - edge)

    @pl.when(group < groups - 1)
    def _():
        greet_group(group + 1, col >= col_tiles - edge, 0)

    base = slabs - 1 + col_tiles - 1
    above = jnp.where(group > 0, jnp.where(col < edge, col_tiles, edge), 0)
    below = jnp.where(group < groups - 1, jnp.where(col >= col_tiles - edge, col_tiles, edge), 0)
    return barrier, base + above + below


def cos_sin(x):
    turn = jnp.floor(x * (2.0 / math.pi) + 0.5)
    r = ((x - turn * 1.5703125) - turn * 4.837512969970703125e-4) - turn * 7.54978995489188216e-8
    z = r * r
    s = ((-1.9515295891e-4 * z + 8.3321608736e-3) * z - 1.6666654611e-1) * z * r + r
    c = ((2.443315711809948e-5 * z - 1.388731625493765e-3) * z + 4.166664568298827e-2) * z * z
    c = c - 0.5 * z + 1.0
    quarter = turn.astype(jnp.int32) & 3
    odd = (quarter & 1) == 1
    cos = jnp.where(odd, s, c)
    sin = jnp.where(odd, c, s)
    cos = jnp.where((quarter == 1) | (quarter == 2), -cos, cos)
    sin = jnp.where(quarter >= 2, -sin, sin)
    return cos, sin


def split(x):
    high = x.astype(BF16)
    return high, (x - high.astype(F32)).astype(BF16)


def mm(a, b):
    return jnp.dot(a, b, preferred_element_type=F32)


def grad_kernel(
    slabs, strips, shear_ref, pos_ref, vol_any, probe_any, meas_any, tab_any, out_ref,
    vol_ref, probe_ref, meas_ref, tab_ref, load_sem,
    part, slab_in, proj, land, land_edge,
    cosf, sinf, acc, grad_ref, grad_land, grad_edge, total, own, grad_slab,
    slab_send, slab_recv, send, recv, edge_send, edge_recv,
    b_slab_send, b_slab_recv, b_send, b_recv, b_edge_send, b_edge_recv,
):
    pairs_of = (
        (vol_any, vol_ref), (probe_any, probe_ref), (meas_any, meas_ref), (tab_any, tab_ref),
    )
    loads = [pltpu.make_async_copy(a, b, load_sem.at[k]) for k, (a, b) in enumerate(pairs_of)]
    for load in loads:
        load.start()
    depth, rows, width = vol_ref.shape
    wide = width + 2 * RIM
    col_tiles = width // TILE_W
    groups = strips // col_tiles
    edge = RIM // rows
    slots = col_tiles + 2 * edge
    halves = WIN // PATCH
    cut_rows = rows // CUTS
    cuts_at = [pl.ds(h * cut_rows, cut_rows) for h in range(CUTS)]
    slab, strip = place()
    group, col = strip // col_tiles, strip % col_tiles
    barrier, peers = greet(slab, strip, slabs, strips, col_tiles, edge)
    lane = lax.broadcasted_iota(jnp.int32, (rows, wide), 1)
    inside = (lane >= RIM) & (lane < RIM + width)
    zeros = jnp.zeros((rows, 2 * RIM), F32)

    def put(field, at, value):
        for h in range(halves):
            field[h, at, :] = value[:, h * PATCH : (h + 1) * PATCH]

    def trig(place_at, phase):
        cos, sin = cos_sin(phase.astype(F32))
        at = pl.ds(pl.multiple_of(place_at * rows, rows), rows)
        put(cosf, at, cos)
        put(sinf, at, sin)

    def partial(view):
        total = jnp.zeros((rows, wide), F32)
        for z in range(depth):
            layer = jnp.concatenate([vol_ref[z].astype(F32), zeros], 1)
            total = total + pltpu.roll(layer, shear_ref[view, z] + RIM, 1)
        return jnp.where(inside, total, 0.0).astype(BF16)

    loads[0].wait()
    copies = []
    for step in range(1, slabs):
        view = lax.rem(slab + step, slabs)
        part[step - 1] = partial(view)
        if step == 1:
            pl.semaphore_wait(barrier, peers)
        for h, at in enumerate(cuts_at):
            copy = pltpu.make_async_remote_copy(
                src_ref=part.at[step - 1, at], dst_ref=slab_in.at[step - 1, at],
                send_sem=slab_send.at[step - 1, h], recv_sem=slab_recv.at[step - 1, h],
                device_id={"slab": view, "strip": strip}, device_id_type=MESH,
            )
            copy.start()
            copies.append(copy)
    summed = partial(slab).astype(F32)
    if slabs == 1:
        pl.semaphore_wait(barrier, peers)

    def window(tile):
        return pl.ds(pl.multiple_of(tile * TILE_W, TILE_W), WIN)

    top = (col < edge) & (group > 0)
    bottom = (col >= col_tiles - edge) & (group < groups - 1)
    other = jnp.where(col < edge, group - 1, group + 1)
    slot = jnp.where(col < edge, edge + col, col - (col_tiles - edge))

    def edge_copy(tile, h):
        return pltpu.make_async_remote_copy(
            src_ref=proj.at[cuts_at[h], pl.ds(tile * TILE_W, WIN)],
            dst_ref=land_edge.at[slot, cuts_at[h]],
            send_sem=edge_send.at[tile, h], recv_sem=edge_recv.at[slot, h],
            device_id={"slab": slab, "strip": other * col_tiles + tile}, device_id_type=MESH,
        )

    group_copies = [[] for _ in range(col_tiles)]

    def send_windows(h):
        @pl.when(top | bottom)
        def _():
            for tile in range(col_tiles):
                edge_copy(tile, h).start()

        for step in range(1, col_tiles):
            tile = lax.rem(col + step, col_tiles)
            copy = pltpu.make_async_remote_copy(
                src_ref=proj.at[cuts_at[h], window(tile)],
                dst_ref=land.at[step - 1, cuts_at[h]],
                send_sem=send.at[step - 1, h], recv_sem=recv.at[step - 1, h],
                device_id={"slab": slab, "strip": group * col_tiles + tile}, device_id_type=MESH,
            )
            copy.start()
            group_copies[step].append(copy)

    for h, at in enumerate(cuts_at):
        value = summed[h * cut_rows : (h + 1) * cut_rows]
        for step in range(1, slabs):
            copies[CUTS * (step - 1) + h].wait_recv()
            value = value + slab_in[step - 1, at].astype(F32)
        proj[at] = value.astype(BF16)
        send_windows(h)
    trig(edge + col, proj[:, window(col)])
    acc[...] = jnp.zeros_like(acc)
    for step in range(1, col_tiles):
        for copy in group_copies[step]:
            copy.wait_recv()
        trig(edge + lax.rem(col + col_tiles - step, col_tiles), land[step - 1])

    def edge_in(first, place_at, has):
        @pl.when(has)
        def _():
            for k in range(edge):
                for h, at in enumerate(cuts_at):
                    pltpu.make_async_remote_copy(
                        src_ref=proj.at[at, pl.ds(0, WIN)],
                        dst_ref=land_edge.at[first + k, at],
                        send_sem=edge_send.at[0, h], recv_sem=edge_recv.at[first + k, h],
                        device_id={"slab": slab, "strip": other * col_tiles},
                        device_id_type=MESH,
                    ).wait_recv()
                trig(place_at + k, land_edge[first + k])

        @pl.when(jnp.logical_not(has))
        def _():
            for k in range(edge):
                at = pl.ds((place_at + k) * rows, rows)
                put(cosf, at, jnp.ones((rows, WIN), F32))
                put(sinf, at, jnp.zeros((rows, WIN), F32))

    edge_in(0, 0, group > 0)
    edge_in(edge, edge + col_tiles, group < groups - 1)

    for load in loads[1:]:
        load.wait()
    count = meas_ref.shape[0]

    def right(x, which):
        return mm(x.astype(BF16), tab_ref[2 * which])

    def left(which, x):
        return mm(tab_ref[2 * which], x.astype(BF16))

    def right3(x, which):
        high, low = split(x)
        t_high, t_low = tab_ref[2 * which], tab_ref[2 * which + 1]
        return mm(high, t_high) + (mm(low, t_high) + mm(high, t_low))

    def left3(which, x):
        high, low = split(x)
        t_high, t_low = tab_ref[2 * which], tab_ref[2 * which + 1]
        return mm(t_high, high) + (mm(t_high, low) + mm(t_low, high))

    def regroup(x):
        return jnp.concatenate(
            [
                jnp.concatenate([x[:PATCH, :PATCH], x[PATCH:, :PATCH]], 1),
                jnp.concatenate([x[:PATCH, PATCH:], x[PATCH:, PATCH:]], 1),
            ],
            0,
        )

    def cut(field, row, by):
        strips = [field[h, pl.ds(row, PATCH), :] for h in range(halves)]
        return pltpu.roll(jnp.concatenate(strips, 1), by, 1)[:, :PATCH]

    def pairs(j, _):
        probe_re, probe_im = probe_ref[0], probe_ref[1]
        members = [PAIRS * j + u for u in range(PAIRS)]
        where, cuts, halves_in = [], [], []
        for i in members:
            waves = []
            for k in range(2):
                row = pos_ref[0, 2 * i + k] + RIM
                lane = pos_ref[1, 2 * i + k] + RIM
                back_by = (WIN - lane) & (WIN - 1)
                cos = cut(cosf, row, back_by)
                sin = cut(sinf, row, back_by)
                where.append((row, lane))
                cuts.append((cos, sin))
                wave_re = probe_re * cos - probe_im * sin
                wave_im = probe_re * sin + probe_im * cos
                waves.append(jnp.concatenate([wave_re, wave_im], 1))
            halves_in.append(jnp.concatenate(waves, 0))
        half = [regroup(right3(x, 0)) for x in halves_in]
        far = [left3(1, x) for x in half]
        weighted = []
        for i, x in zip(members, far):
            far_re, far_im = x[:PATCH], x[PATCH:]
            meas = jnp.concatenate([meas_ref[2 * i], meas_ref[2 * i + 1]], 1).astype(F32)
            weight = GRAD_SCALE * (far_re * far_re + far_im * far_im - meas)
            weighted.append(jnp.concatenate([weight * far_re, weight * far_im], 0))
        half = [regroup(left(0, x)) for x in weighted]
        back = [right(x, 1) for x in half]
        placed, rows_at = [], []
        for u in range(2 * PAIRS):
            row, lane = where[u]
            cos, sin = cuts[u]
            k = u % 2
            back_re = back[u // 2][k * PATCH : (k + 1) * PATCH, :PATCH]
            back_im = back[u // 2][k * PATCH : (k + 1) * PATCH, PATCH:]
            grad_re = probe_re * back_re + probe_im * back_im
            grad_im = probe_re * back_im - probe_im * back_re
            grad = cos * grad_im - sin * grad_re
            grad = jnp.concatenate([grad, jnp.zeros_like(grad)], 1)
            placed.append(pltpu.roll(grad, lane, 1).astype(BF16))
            rows_at.append(lax.broadcasted_iota(jnp.int32, (1, PATCH), 1) + row)
        row_at = jnp.concatenate(rows_at, 1)
        ext_row = lax.broadcasted_iota(jnp.int32, (slots * rows, row_at.shape[1]), 0)
        select = jnp.where(ext_row == row_at, 1.0, 0.0).astype(BF16)
        acc[...] = acc[...] + mm(select, jnp.concatenate(placed, 0))
        return 0

    lax.fori_loop(0, count // (2 * PAIRS), pairs, 0)

    grad_ref[...] = acc[...].astype(BF16).reshape(slots, rows, WIN)

    def b_edge_copy(h, k, to_group, source, owner):
        return pltpu.make_async_remote_copy(
            src_ref=grad_ref.at[source, cuts_at[h]], dst_ref=grad_edge.at[col, cuts_at[h]],
            send_sem=b_edge_send.at[k, h], recv_sem=b_edge_recv.at[col, h],
            device_id={"slab": slab, "strip": to_group * col_tiles + owner}, device_id_type=MESH,
        )

    def b_edge_copies(h, act):
        @pl.when(group > 0)
        def _():
            for k in range(edge):
                act(b_edge_copy(h, k, group - 1, k, col_tiles - edge + k))

        @pl.when(group < groups - 1)
        def _():
            for k in range(edge):
                act(b_edge_copy(h, edge + k, group + 1, edge + col_tiles + k, k))

    b_group_copies = []
    for h, at in enumerate(cuts_at):
        b_edge_copies(h, lambda copy: copy.start())
        b_group_copies.append([])
        for step in range(1, col_tiles):
            tile = lax.rem(col + step, col_tiles)
            copy = pltpu.make_async_remote_copy(
                src_ref=grad_ref.at[edge + tile, at], dst_ref=grad_land.at[step - 1, at],
                send_sem=b_send.at[step - 1, h], recv_sem=b_recv.at[step - 1, h],
                device_id={"slab": slab, "strip": group * col_tiles + tile}, device_id_type=MESH,
            )
            copy.start()
            b_group_copies[h].append(copy)
    total[...] = jnp.zeros((rows, wide), F32)
    total[:, window(col)] = total[:, window(col)] + grad_ref[edge + col].astype(F32)
    b_copies = []
    for h, at in enumerate(cuts_at):
        for step in range(1, col_tiles):
            b_group_copies[h][step - 1].wait_recv()
            to = window(lax.rem(col + col_tiles - step, col_tiles))
            total[at, to] = total[at, to] + grad_land[step - 1, at].astype(F32)

        @pl.when(top | bottom)
        def _():
            for tile in range(col_tiles):
                pltpu.make_async_remote_copy(
                    src_ref=grad_ref.at[0, at], dst_ref=grad_edge.at[tile, at],
                    send_sem=b_edge_send.at[0, h], recv_sem=b_edge_recv.at[tile, h],
                    device_id={"slab": slab, "strip": other * col_tiles + tile},
                    device_id_type=MESH,
                ).wait_recv()
                to = window(tile)
                total[at, to] = total[at, to] + grad_edge[tile, at].astype(F32)

        own[at] = jnp.where(inside[:cut_rows], total[at], 0.0).astype(BF16)
        for step in range(1, slabs):
            copy = pltpu.make_async_remote_copy(
                src_ref=own.at[at], dst_ref=grad_slab.at[step - 1, at],
                send_sem=b_slab_send.at[step - 1, h], recv_sem=b_slab_recv.at[step - 1, h],
                device_id={"slab": lax.rem(slab + step, slabs), "strip": strip},
                device_id_type=MESH,
            )
            copy.start()
            b_copies.append(copy)

    out_ref[slab] = own[...]
    for copy in b_copies:
        copy.wait_recv()
    for step in range(1, slabs):
        out_ref[lax.rem(slab + slabs - step, slabs)] = grad_slab[step - 1]
    for copy in b_copies + sum(b_group_copies, []):
        copy.wait_send()
    for h in range(CUTS):
        b_edge_copies(h, lambda copy: copy.wait_send())
    for copy in copies + sum(group_copies, []):
        copy.wait_send()

    @pl.when(top | bottom)
    def _():
        for tile in range(col_tiles):
            for h in range(CUTS):
                edge_copy(tile, h).wait_send()


def spread_kernel(shear_ref, fields_ref, out_ref):
    depth, rows, width = out_ref.shape
    views, _, wide = fields_ref.shape
    for z in range(depth):
        result = jnp.zeros((rows, width), F32)
        for view in range(views):
            by = lax.rem(wide - RIM - shear_ref[view, z], wide)
            result = result + pltpu.roll(fields_ref[view].astype(F32), by, 1)[:, :width]
        out_ref[z] = result.astype(BF16)


def local(slabs, strips, volume, shear, probe, positions, measured):
    _, rows, width = volume.shape
    col_tiles = width // TILE_W
    wide = width + 2 * RIM
    edge = RIM // rows
    slots = col_tiles + 2 * edge
    others = max(slabs - 1, 1)
    vmem = pl.BlockSpec(memory_space=pltpu.VMEM)
    smem = pl.BlockSpec(memory_space=pltpu.SMEM)
    anywhere = pl.BlockSpec(memory_space=pl.ANY)
    dma = pltpu.SemaphoreType.DMA
    tables = jnp.asarray(dft_tables())
    patches = measured[0, 0]
    fields = pl.pallas_call(
        functools.partial(grad_kernel, slabs, strips),
        out_shape=jax.ShapeDtypeStruct((slabs, rows, wide), BF16),
        in_specs=[smem, smem, anywhere, anywhere, anywhere, anywhere],
        out_specs=vmem,
        scratch_shapes=[
            pltpu.VMEM(volume.shape, BF16),
            pltpu.VMEM(probe.shape, F32),
            pltpu.VMEM(patches.shape, BF16),
            pltpu.VMEM(tables.shape, BF16),
            dma((4,)),
            pltpu.VMEM((others, rows, wide), BF16),
            pltpu.VMEM((others, rows, wide), BF16),
            pltpu.VMEM((rows, wide), BF16),
            pltpu.VMEM((col_tiles - 1, rows, WIN), BF16),
            pltpu.VMEM((2 * edge, rows, WIN), BF16),
            pltpu.VMEM((WIN // PATCH, slots * rows, PATCH), F32),
            pltpu.VMEM((WIN // PATCH, slots * rows, PATCH), F32),
            pltpu.VMEM((slots * rows, WIN), F32),
            pltpu.VMEM((slots, rows, WIN), BF16),
            pltpu.VMEM((col_tiles - 1, rows, WIN), BF16),
            pltpu.VMEM((col_tiles, rows, WIN), BF16),
            pltpu.VMEM((rows, wide), F32),
            pltpu.VMEM((rows, wide), BF16),
            pltpu.VMEM((others, rows, wide), BF16),
            dma((others, CUTS)), dma((others, CUTS)),
            dma((col_tiles - 1, CUTS)), dma((col_tiles - 1, CUTS)),
            dma((col_tiles, CUTS)), dma((2 * edge, CUTS)),
            dma((others, CUTS)), dma((others, CUTS)),
            dma((col_tiles - 1, CUTS)), dma((col_tiles - 1, CUTS)),
            dma((2 * edge, CUTS)), dma((col_tiles, CUTS)),
        ],
        compiler_params=pltpu.CompilerParams(collective_id=0, has_side_effects=True),
        name="gradient",
    )(shear, positions[0, 0].T, volume, probe, patches, tables)
    return pl.pallas_call(
        spread_kernel,
        out_shape=jax.ShapeDtypeStruct(volume.shape, BF16),
        in_specs=[smem, vmem],
        out_specs=vmem,
        name="spread",
    )(shear, fields)


def solution(mesh):
    placed = (
        P("slab", "strip", None),
        P(None, "slab"),
        P(),
        P("slab", "strip", None, None),
        P("slab", "strip", None, None, None),
    )
    return jax.shard_map(
        functools.partial(local, mesh.shape["slab"], mesh.shape["strip"]),
        mesh=mesh, in_specs=placed, out_specs=P("slab", "strip", None), check_vma=False,
    )
```
